32 devices in a mesh: fsdp: 4 (over y, x), seq: 8 (over z, core).
Axes of the slice: x: 2, y: 2, z: 4, core: 2. Of those that a mesh axis runs over, the one named last changes fastest.
Arguments:
- images: bfloat16 [4, 1024, 1024], P('fsdp', 'seq'), may hold values from -7 to 7
- valid_mask: int32 [4, 1024], P('fsdp'), may hold values from 0 to 1, as said below
- ln1_gain: bfloat16 [1, 1024], P(None, ('fsdp', 'seq')), may hold values from 0.25 to 1.75
- ln1_bias: bfloat16 [1, 1024], P(None, ('fsdp', 'seq')), may hold values from -4 to 4
- qkv_weight: bfloat16 [1, 1024, 3072], P(None, ('fsdp', 'seq')), may hold values from -4 to 4
- q_bias: bfloat16 [1, 1024], P(None, ('fsdp', 'seq')), may hold values from -6 to 6
- v_bias: bfloat16 [1, 1024], P(None, ('fsdp', 'seq')), may hold values from -0.75 to 0.75
- proj_weight: bfloat16 [1, 1024, 1024], P(None, None, ('fsdp', 'seq')), may hold values from -12 to 12
- proj_bias: bfloat16 [1, 1024], P(None, ('fsdp', 'seq')), may hold values from -4 to 4
- ln2_gain: bfloat16 [1, 1024], P(None, ('fsdp', 'seq')), may hold values from 0.25 to 1.75
- ln2_bias: bfloat16 [1, 1024], P(None, ('fsdp', 'seq')), may hold values from -4 to 4
- fc1_weight: bfloat16 [1, 1024, 4096], P(None, ('fsdp', 'seq')), may hold values from -0.1875 to 0.1875
- fc1_bias: bfloat16 [1, 4096], P(None, ('fsdp', 'seq')), may hold values from -4 to 4
- fc2_weight: bfloat16 [1, 4096, 1024], P(None, None, ('fsdp', 'seq')), may hold values from -0.09375 to 0.09375
- fc2_bias: bfloat16 [1, 1024], P(None, ('fsdp', 'seq')), may hold values from -4 to 4
- out_grad: float32 [4, 1024, 1024], P('fsdp', 'seq'), may hold values from -6 to 6
Outputs:
- block_out: bfloat16 [4, 1024, 1024], P('fsdp', 'seq')
- images_grad: float32 [4, 1024, 1024], P('fsdp', 'seq')
- ln1_gain_grad: float32 [1, 1024], P(None, ('fsdp', 'seq'))
- ln1_bias_grad: float32 [1, 1024], P(None, ('fsdp', 'seq'))
- qkv_weight_grad: float32 [1, 1024, 3072], P(None, ('fsdp', 'seq'))
- q_bias_grad: float32 [1, 1024], P(None, ('fsdp', 'seq'))
- v_bias_grad: float32 [1, 1024], P(None, ('fsdp', 'seq'))
- proj_weight_grad: float32 [1, 1024, 1024], P(None, None, ('fsdp', 'seq'))
- proj_bias_grad: float32 [1, 1024], P(None, ('fsdp', 'seq'))
- ln2_gain_grad: float32 [1, 1024], P(None, ('fsdp', 'seq'))
- ln2_bias_grad: float32 [1, 1024], P(None, ('fsdp', 'seq'))
- fc1_weight_grad: float32 [1, 1024, 4096], P(None, ('fsdp', 'seq'))
- fc1_bias_grad: float32 [1, 4096], P(None, ('fsdp', 'seq'))
- fc2_weight_grad: float32 [1, 4096, 1024], P(None, None, ('fsdp', 'seq'))
- fc2_bias_grad: float32 [1, 1024], P(None, ('fsdp', 'seq'))
The draws below stay inside these ranges and needn't reach their ends.
Inputs may be any that keep to these rules, and one draw needn't show every extreme that they name: valid_mask is 1 on the first tokens of each image and 0 on the rest; at least one and at most 256 of an image's last tokens are 0.
All inputs are finite; a program needn't handle non-finite values.
Results may differ from the reference program's by a relative error of at most 0.012.
Values may be sent and summed in bfloat16 or wider, within the bound.
No kernel may reach another device: no remote copies, remote signals or barrier semaphores. Data moves between devices by JAX's collectives and lax.ppermute only.
A program may use at most 192 MiB of HBM per device.

```python
import jax
import jax.numpy as jnp
from jax import lax

D = 1024
HEADS = 16
HD = 64
FF = 4096
LAYERS = 1
TOK_DEV = 128
IMAGES = 4
TOKENS = 1024


def draw_images(key, part):
    drawn = jax.random.truncated_normal(key, -6.0, 6.0, (IMAGES, TOKENS, D), jnp.float32)
    return drawn.astype(jnp.bfloat16)


def draw_valid_mask(key, part):
    padding = jax.random.randint(key, (IMAGES,), 1, 2 * TOK_DEV + 1)
    image_order = jnp.arange(IMAGES)
    padding = jnp.where(image_order == 0, 2 * TOK_DEV, jnp.where(image_order == IMAGES - 1, 1, padding))
    position = jnp.arange(TOKENS)
    return (position[None, :] < (TOKENS - padding)[:, None]).astype(jnp.int32)


def draw_qkv_weight(key, part):
    return (jax.random.truncated_normal(key, -5.0, 5.0, (LAYERS, D, 3 * D), jnp.float32) * D ** (-0.5)).astype(jnp.bfloat16)


def draw_proj_weight(key, part):
    baseline = jax.random.truncated_normal(key, -4.0, 4.0, (LAYERS, D, D), jnp.float32) * D ** (-0.5)
    return (baseline * (0.5 * TOKENS ** 0.5)).astype(jnp.bfloat16)


def block_levels(key, extent, split, least, top_value):
    loudness, own = 1.0, jax.random.fold_in(key, 6)
    for dim, blocks in split:
        draws = jnp.exp(jax.random.uniform(jax.random.fold_in(own, dim), (blocks,), jnp.float32, least / len(split), top_value / len(split)))
        loudness = loudness * jnp.repeat(draws, extent[dim] // blocks).reshape([-1 if axis == dim else 1 for axis in range(len(extent))])
    return loudness


def gaussian(key, dims, width, bound, pieces=(), held_as=jnp.bfloat16):
    values = jax.random.normal(key, dims, jnp.float32) * width
    if len(pieces) > 0:
        values = block_levels(key, dims, pieces, -0.22, 0.18) * values
    return jnp.clip(values, min=-bound, max=bound).astype(held_as)


def setup_inputs(seed: int = 0) -> dict:
    streams_of = jax.random.split(jax.random.key(seed), 17)
    return {
        "images": draw_images(jax.random.fold_in(streams_of[16], 71), 0),
        "valid_mask": draw_valid_mask(jax.random.fold_in(streams_of[16], 71), 0),
        "ln1_gain": jnp.clip(1.0 + 0.15 * jax.random.normal(streams_of[2], (LAYERS, D), jnp.float32), 0.25, 1.75).astype(jnp.bfloat16),
        "ln1_bias": gaussian(streams_of[3], (LAYERS, D), 0.3, 4.0, ((1, 32),)),
        "qkv_weight": draw_qkv_weight(jax.random.fold_in(streams_of[16], 71), 0),
        "q_bias": gaussian(streams_of[5], (LAYERS, D), 0.5, 6.0, ((1, 32),)),
        "v_bias": gaussian(streams_of[6], (LAYERS, D), 0.05, 0.75, ((1, 32),)),
        "proj_weight": draw_proj_weight(jax.random.fold_in(streams_of[16], 71), 0),
        "proj_bias": gaussian(streams_of[8], (LAYERS, D), 0.3, 4.0, ((1, 32),)),
        "ln2_gain": jnp.clip(1.0 + 0.15 * jax.random.normal(streams_of[9], (LAYERS, D), jnp.float32), 0.25, 1.75).astype(jnp.bfloat16),
        "ln2_bias": gaussian(streams_of[10], (LAYERS, D), 0.3, 4.0, ((1, 32),)),
        "fc1_weight": gaussian(streams_of[11], (LAYERS, D, FF), D ** -0.5, 0.1875, ((1, 32),)),
        "fc1_bias": gaussian(streams_of[12], (LAYERS, FF), 0.3, 4.0, ((1, 32),)),
        "fc2_weight": gaussian(streams_of[13], (LAYERS, FF, D), FF ** -0.5, 0.09375, ((2, 32),)),
        "fc2_bias": gaussian(streams_of[14], (LAYERS, D), 0.3, 4.0, ((1, 32),)),
        "out_grad": gaussian(streams_of[15], (IMAGES, TOKENS, D), 1.0, 6.0, ((0, 4), (1, 8)), jnp.float32),
    }


epsilon = 1e-06
masked_score = -1e+30
root_half = 0.7071067811865476
inv_root_tau = 0.3989422804014327

def normalize(hidden):
    center = hidden - lax.optimization_barrier(jnp.mean(hidden, axis=-1, keepdims=True))
    spread = lax.rsqrt(lax.optimization_barrier(jnp.mean(center * center, axis=-1, keepdims=True)) + epsilon)
    return (center * spread, spread)

def norm_back(grad_in, normed, spread, gain_vec):
    scaled = grad_in * gain_vec.astype(jnp.float32)
    return spread * (scaled - lax.optimization_barrier(jnp.mean(scaled, axis=-1, keepdims=True)) - normed * lax.optimization_barrier(jnp.mean(scaled * normed, axis=-1, keepdims=True)))

def gelu_value(pre_act):
    return 0.5 * pre_act * (1.0 + lax.erf(pre_act * root_half))

def gelu_slope(pre_act):
    return 0.5 * (1.0 + lax.erf(pre_act * root_half)) + pre_act * inv_root_tau * jnp.exp(-0.5 * pre_act * pre_act)

def block_scores(query_rows, keys_in, valid_keys):
    scores = 0.125 * jnp.dot(query_rows, keys_in.T, preferred_element_type=jnp.float32)
    return jnp.where(valid_keys[None, :], scores, masked_score)

def head_forward(queries, keys_in, values, valid_keys):
    row_count, head_width = queries.shape
    row_block = min(512, row_count)

    def one_block(query_rows):
        scores = block_scores(query_rows, keys_in, valid_keys)
        row_top = lax.optimization_barrier(jnp.max(scores, axis=1, keepdims=True))
        log_total = row_top + jnp.log(lax.optimization_barrier(jnp.sum(jnp.exp(scores - row_top), axis=1, keepdims=True)))
        prob_rows = jnp.exp(scores - log_total).astype(jnp.bfloat16)
        outputs = jnp.dot(prob_rows, values, preferred_element_type=jnp.float32).astype(jnp.bfloat16)
        return (outputs, log_total[:, 0])
    outputs, log_total = lax.map(one_block, queries.reshape(row_count // row_block, row_block, head_width))
    return (outputs.reshape(row_count, head_width), log_total.reshape(row_count))

def head_backward(queries, keys_in, values, valid_keys, log_total, grad_out):
    row_count, head_width = queries.shape
    row_block = min(512, row_count)
    blocks = row_count // row_block

    def one_block(running, entries):
        key_sum, value_sum = running
        query_rows, log_rows, grad_rows = entries
        prob_rows = jnp.exp(block_scores(query_rows, keys_in, valid_keys) - log_rows[:, None])
        value_sum = value_sum + jnp.dot(prob_rows.astype(jnp.bfloat16).T, grad_rows, preferred_element_type=jnp.float32)
        prob_grad = jnp.dot(grad_rows, values.T, preferred_element_type=jnp.float32)
        centered = prob_grad - lax.optimization_barrier(jnp.sum(prob_rows * prob_grad, axis=1, keepdims=True))
        score_grad = (prob_rows * centered).astype(jnp.bfloat16)
        query_grad = (0.125 * jnp.dot(score_grad, keys_in, preferred_element_type=jnp.float32)).astype(jnp.bfloat16)
        key_sum = key_sum + jnp.dot(score_grad.T, query_rows, preferred_element_type=jnp.float32)
        return ((key_sum, value_sum), query_grad)
    zero_sum = jnp.zeros((row_count, head_width), jnp.float32)
    (key_sum, value_sum), query_grad = lax.scan(one_block, (zero_sum, zero_sum), (queries.reshape(blocks, row_block, head_width), log_total.reshape(blocks, row_block), grad_out.reshape(blocks, row_block, head_width)))
    return (query_grad.reshape(row_count, head_width), (0.125 * key_sum).astype(jnp.bfloat16), value_sum.astype(jnp.bfloat16))

def split_heads(matrix):
    return matrix.reshape(matrix.shape[0], HEADS, HD).transpose(1, 0, 2)

def merge_heads(stacked):
    return stacked.transpose(1, 0, 2).reshape(stacked.shape[1], HEADS * HD)

def layer_forward(hidden, params, valid_keys):
    gain_one, shift_one, qkv_mat, query_bias, value_bias, proj_mat, proj_shift, gain_two, shift_two, up_mat, up_shift, down_mat, down_shift = params
    normed_one, spread_one = normalize(hidden)
    attn_in = (normed_one * gain_one.astype(jnp.float32) + shift_one.astype(jnp.float32)).astype(jnp.bfloat16)
    qkv_rows = jnp.dot(attn_in, qkv_mat, preferred_element_type=jnp.float32)
    queries = (qkv_rows[:, :D] + query_bias.astype(jnp.float32)).astype(jnp.bfloat16)
    keys_in = qkv_rows[:, D:2 * D].astype(jnp.bfloat16)
    values = (qkv_rows[:, 2 * D:] + value_bias.astype(jnp.float32)).astype(jnp.bfloat16)
    head_out, log_total = lax.map(lambda entries: head_forward(entries[0], entries[1], entries[2], valid_keys), (split_heads(queries), split_heads(keys_in), split_heads(values)))
    attended = merge_heads(head_out)
    after_attn = hidden + jnp.dot(attended, proj_mat, preferred_element_type=jnp.float32) + proj_shift.astype(jnp.float32)
    normed_two, spread_two = normalize(after_attn)
    mlp_in = (normed_two * gain_two.astype(jnp.float32) + shift_two.astype(jnp.float32)).astype(jnp.bfloat16)
    pre_act = jnp.dot(mlp_in, up_mat, preferred_element_type=jnp.float32) + up_shift.astype(jnp.float32)
    activated = gelu_value(pre_act).astype(jnp.bfloat16)
    result = after_attn + jnp.dot(activated, down_mat, preferred_element_type=jnp.float32) + down_shift.astype(jnp.float32)
    kept_acts = (normed_one, spread_one, attn_in, queries, keys_in, values, log_total, attended, normed_two, spread_two, mlp_in, pre_act, activated)
    return (result, kept_acts)

def layer_backward(grad_out, params, kept_acts, valid_keys):
    gain_one, shift_one, qkv_mat, query_bias, value_bias, proj_mat, proj_shift, gain_two, shift_two, up_mat, up_shift, down_mat, down_shift = params
    normed_one, spread_one, attn_in, queries, keys_in, values, log_total, attended, normed_two, spread_two, mlp_in, pre_act, activated = kept_acts
    grad_low = grad_out.astype(jnp.bfloat16)
    down_grad = jnp.dot(activated.T, grad_low, preferred_element_type=jnp.float32)
    down_shift_grad = lax.optimization_barrier(jnp.sum(grad_out, axis=0))
    pre_grad = jnp.dot(grad_low, down_mat.T, preferred_element_type=jnp.float32) * gelu_slope(pre_act)
    up_shift_grad = lax.optimization_barrier(jnp.sum(pre_grad, axis=0))
    pre_low = pre_grad.astype(jnp.bfloat16)
    up_grad = jnp.dot(mlp_in.T, pre_low, preferred_element_type=jnp.float32)
    mlp_grad = jnp.dot(pre_low, up_mat.T, preferred_element_type=jnp.float32)
    gain_two_grad = lax.optimization_barrier(jnp.sum(mlp_grad * normed_two, axis=0))
    shift_two_grad = lax.optimization_barrier(jnp.sum(mlp_grad, axis=0))
    mid_grad = grad_out + norm_back(mlp_grad, normed_two, spread_two, gain_two)
    mid_low = mid_grad.astype(jnp.bfloat16)
    proj_grad = jnp.dot(attended.T, mid_low, preferred_element_type=jnp.float32)
    proj_shift_grad = lax.optimization_barrier(jnp.sum(mid_grad, axis=0))
    attended_grad = jnp.dot(mid_low, proj_mat.T, preferred_element_type=jnp.float32).astype(jnp.bfloat16)
    query_grad, key_grad, value_grad = lax.map(lambda entries: head_backward(entries[0], entries[1], entries[2], valid_keys, entries[3], entries[4]), (split_heads(queries), split_heads(keys_in), split_heads(values), log_total, split_heads(attended_grad)))
    qkv_grad = jnp.concatenate([merge_heads(query_grad), merge_heads(key_grad), merge_heads(value_grad)], axis=1)
    qkv_mat_grad = jnp.dot(attn_in.T, qkv_grad, preferred_element_type=jnp.float32)
    query_bias_grad = lax.optimization_barrier(jnp.sum(qkv_grad[:, :D].astype(jnp.float32), axis=0))
    value_bias_grad = lax.optimization_barrier(jnp.sum(qkv_grad[:, 2 * D:].astype(jnp.float32), axis=0))
    attn_in_grad = jnp.dot(qkv_grad, qkv_mat.T, preferred_element_type=jnp.float32)
    gain_one_grad = lax.optimization_barrier(jnp.sum(attn_in_grad * normed_one, axis=0))
    shift_one_grad = lax.optimization_barrier(jnp.sum(attn_in_grad, axis=0))
    input_grad = mid_grad + norm_back(attn_in_grad, normed_one, spread_one, gain_one)
    return (input_grad, (gain_one_grad, shift_one_grad, qkv_mat_grad, query_bias_grad, value_bias_grad, proj_grad, proj_shift_grad, gain_two_grad, shift_two_grad, up_grad, up_shift_grad, down_grad, down_shift_grad))

def reference(images, valid_mask, ln1_gain, ln1_bias, qkv_weight, q_bias, v_bias, proj_weight, proj_bias, ln2_gain, ln2_bias, fc1_weight, fc1_bias, fc2_weight, fc2_bias, out_grad):
    weights = (ln1_gain, ln1_bias, qkv_weight, q_bias, v_bias, proj_weight, proj_bias, ln2_gain, ln2_bias, fc1_weight, fc1_bias, fc2_weight, fc2_bias)

    def one_image(totals, entries):
        image, mask_row, cotangent = entries
        valid_keys = mask_row > 0
        hidden = image.astype(jnp.float32)
        kept_list = []
        for layer_pos in range(LAYERS):
            params = tuple((array[layer_pos] for array in weights))
            hidden, kept_acts = layer_forward(hidden, params, valid_keys)
            kept_list.append(kept_acts)
        back_grad = cotangent.astype(jnp.float32)
        new_totals = list(totals)
        for layer_pos in reversed(range(LAYERS)):
            params = tuple((array[layer_pos] for array in weights))
            back_grad, layer_grads = layer_backward(back_grad, params, kept_list[layer_pos], valid_keys)
            new_totals[layer_pos] = tuple((total + piece for total, piece in zip(totals[layer_pos], layer_grads)))
        return (tuple(new_totals), (hidden.astype(jnp.bfloat16), back_grad))
    zero_totals = tuple((tuple((jnp.zeros(array.shape[1:], jnp.float32) for array in weights)) for layer_pos in range(LAYERS)))
    totals, (block_out, images_grad) = lax.scan(one_image, zero_totals, (images, valid_mask, out_grad))
    grads = [jnp.stack([totals[layer_pos][param_pos] for layer_pos in range(LAYERS)]) for param_pos in range(13)]
    return (block_out, images_grad, grads[0], grads[1], grads[2], grads[3], grads[4], grads[5], grads[6], grads[7], grads[8], grads[9], grads[10], grads[11], grads[12])
```

```python
import jax
import jax.numpy as jnp
from jax import lax
from jax.experimental import pallas as pl
from jax.experimental.pallas import tpu as pltpu
from jax.sharding import Mesh
from jax.sharding import PartitionSpec as P

HD = 64

epsilon = 1e-06
masked_score = -1e30
root_half = 0.7071067811865476
inv_root_tau = 0.3989422804014327
f32 = jnp.float32
bf16 = jnp.bfloat16
ALL = ("fsdp", "z", "core")
SEQ = ("z", "core")


def normalize(hidden):
    center = hidden - jnp.mean(hidden, axis=-1, keepdims=True)
    spread = lax.rsqrt(jnp.mean(center * center, axis=-1, keepdims=True) + epsilon)
    return (center * spread, spread)


def norm_back(grad_in, normed, spread, gain_vec):
    scaled = grad_in * gain_vec
    return spread * (
        scaled
        - jnp.mean(scaled, axis=-1, keepdims=True)
        - normed * jnp.mean(scaled * normed, axis=-1, keepdims=True)
    )


def mm(a, b, ca=1, cb=0):
    return lax.dot_general(a, b, (((ca,), (cb,)), ((), ())), preferred_element_type=f32)


def lanes_of(block, head):
    lane = lax.broadcasted_iota(jnp.int32, block.shape, 1)
    return jnp.where(lane // HD == head, block, jnp.zeros_like(block))


def attn_fwd_body(q_ref, k_ref, v_ref, ok_ref, out_ref, log_ref):
    heads = q_ref.shape[1] // HD
    queries = q_ref[...] * 0.125
    keys = k_ref[...]
    values = v_ref[...]
    valid = ok_ref[...] > 0
    tops = []
    logs = []
    for head in range(heads):
        scores = mm(keys, lanes_of(queries, head), 1, 1)
        scores = jnp.where(valid, scores, masked_score)
        top = jnp.max(scores, axis=0, keepdims=True)
        powers = jnp.exp(scores - top)
        total = jnp.sum(powers, axis=0, keepdims=True)
        probs = (powers * (1.0 / total)).astype(bf16)
        mixed = mm(values, probs, 0, 0)
        tops.append(mixed[head * HD : (head + 1) * HD])
        logs.append(top + jnp.log(total))
    out_ref[...] = jnp.concatenate(tops, axis=0).T.astype(bf16)
    log_ref[...] = jnp.concatenate(logs, axis=0)


def attn_bwd_body(
    q_ref, g_ref, log_ref, k_ref, v_ref, ok_ref, dq_ref, dk_ref, dv_ref, dk_acc, dv_acc
):
    heads = q_ref.shape[1] // HD
    step = pl.program_id(0)

    @pl.when(step == 0)
    def _():
        dk_acc[...] = jnp.zeros_like(dk_acc)
        dv_acc[...] = jnp.zeros_like(dv_acc)

    queries = q_ref[...] * 0.125
    grads = g_ref[...]
    keys = k_ref[...]
    values = v_ref[...]
    valid = ok_ref[...] > 0
    logs = log_ref[...]
    parts = []
    key_sum = dk_acc[...]
    value_sum = dv_acc[...]
    for head in range(heads):
        q_head = lanes_of(queries, head)
        g_head = lanes_of(grads, head)
        scores = mm(keys, q_head, 1, 1)
        scores = jnp.where(valid, scores, masked_score)
        weights = jnp.exp(scores - logs[head : head + 1])
        prob_grad = mm(values, g_head, 1, 1)
        delta = jnp.sum(weights * prob_grad, axis=0, keepdims=True)
        score_grad = (weights * (prob_grad - delta)).astype(bf16)
        value_sum = value_sum + mm(weights.astype(bf16), g_head)
        key_sum = key_sum + mm(score_grad, q_head)
        mixed = mm(keys, score_grad, 0, 0)
        parts.append(mixed[head * HD : (head + 1) * HD])
    dk_acc[...] = key_sum
    dv_acc[...] = value_sum
    dq_ref[...] = (0.125 * jnp.concatenate(parts, axis=0).T).astype(bf16)

    @pl.when(step == pl.num_programs(0) - 1)
    def _():
        dk_ref[...] = dk_acc[...].astype(bf16)
        dv_ref[...] = dv_acc[...].astype(bf16)


def attn_fwd(q, k, v, valid_col):
    n, w = q.shape
    heads = w // HD
    qb = min(256, n)
    whole = lambda i: (0, 0)
    rows = lambda i: (i, 0)
    return pl.pallas_call(
        attn_fwd_body,
        grid=(n // qb,),
        in_specs=[
            pl.BlockSpec((qb, w), rows),
            pl.BlockSpec((n, w), whole),
            pl.BlockSpec((n, w), whole),
            pl.BlockSpec((n, 1), whole),
        ],
        out_specs=[pl.BlockSpec((qb, w), rows), pl.BlockSpec((heads, qb), lambda i: (0, i))],
        out_shape=[
            jax.ShapeDtypeStruct((n, w), bf16),
            jax.ShapeDtypeStruct((heads, n), f32),
        ],
        name="attn_fwd",
    )(q, k, v, valid_col)


def attn_bwd(q, grad, logs, k, v, valid_col):
    n, w = q.shape
    heads = w // HD
    qb = min(256, n)
    whole = lambda i: (0, 0)
    rows = lambda i: (i, 0)
    return pl.pallas_call(
        attn_bwd_body,
        grid=(n // qb,),
        in_specs=[
            pl.BlockSpec((qb, w), rows),
            pl.BlockSpec((qb, w), rows),
            pl.BlockSpec((heads, qb), lambda i: (0, i)),
            pl.BlockSpec((n, w), whole),
            pl.BlockSpec((n, w), whole),
            pl.BlockSpec((n, 1), whole),
        ],
        out_specs=[
            pl.BlockSpec((qb, w), rows),
            pl.BlockSpec((n, w), whole),
            pl.BlockSpec((n, w), whole),
        ],
        out_shape=[jax.ShapeDtypeStruct((n, w), bf16)] * 3,
        scratch_shapes=[pltpu.VMEM((n, w), f32), pltpu.VMEM((n, w), f32)],
        name="attn_bwd",
    )(q, grad, logs, k, v, valid_col)


def make_shards(F, Z):
    S = 2 * Z
    N_DEV = F * S
    PL = 2 * F

    def swap(x, kf=0, kz=0, kc=0):
        pairs = []
        for f in range(F):
            for z in range(Z):
                for c in range(2):
                    src = (f * Z + z) * 2 + c
                    pairs.append((src, ((f ^ kf) * Z + (z ^ kz)) * 2 + (c ^ kc)))
        return lax.ppermute(x, ALL, pairs)

    def reorder(x, index, axis=0):
        size = x.shape[axis]
        shape = x.shape
        for bit in range(size.bit_length() - 1):
            low = 1 << bit
            split = x.reshape(shape[:axis] + (size // (2 * low), 2, low) + shape[axis + 1 :])
            flipped = jnp.flip(split, axis=axis + 1)
            x = jnp.where((index >> bit) & 1 == 1, flipped, split).reshape(shape)
        return x

    def gather_seq(x):
        out = []
        for kz in range(Z):
            block = x if kz == 0 else swap(x, kz=kz)
            out += [block, swap(block, kc=1)]
        return jnp.concatenate(out, axis=0)

    def gather_plane(x):
        out = []
        for kf in range(F):
            block = x if kf == 0 else swap(x, kf=kf)
            out += [block, swap(block, kc=1)]
        return jnp.concatenate(out, axis=0)

    def scatter_sum(partial, outer, axis_name):
        partial = partial.astype(bf16).reshape(outer, 2, -1, partial.shape[-1])
        other = swap(partial[:, 1], kc=1)
        half = partial[:, 0].astype(f32) + other.astype(f32)
        low = half[1:].astype(bf16)
        total = half[0]
        for k in range(1, outer):
            total = total + swap(low[k - 1], **{axis_name: k}).astype(f32)
        return total

    def exchange(x, axes):
        return lax.all_to_all(x, axes, split_axis=0, concat_axis=0, tiled=True)

    def shards(
        images,
        valid_mask,
        ln1_gain,
        ln1_bias,
        qkv_weight,
        q_bias,
        v_bias,
        proj_weight,
        proj_bias,
        ln2_gain,
        ln2_bias,
        fc1_weight,
        fc1_bias,
        fc2_weight,
        fc2_bias,
        out_grad,
    ):
        _, T, D = images.shape
        R = D // N_DEV
        FF = fc1_weight.shape[2]
        W = D // S
        B = FF // PL
        Q = FF // D
        N = S * T
        fi = lax.axis_index("fsdp")
        zi = lax.axis_index("z")
        ci = lax.axis_index("core")
        si = zi * 2 + ci
        pi = fi * 2 + ci

        x_own = images[0]
        grad_own = out_grad[0]
        x_all = gather_seq(x_own)

        w_qkv = qkv_weight[0].reshape(R, 3, S, W).transpose(2, 0, 1, 3).reshape(1, S, R, 3 * W)
        w_qkv = jnp.broadcast_to(w_qkv, (F, S, R, 3 * W)).reshape(N_DEV, R, 3 * W)
        w_qkv = exchange(w_qkv, ALL).reshape(D, 3 * W)

        vecs = [ln1_gain, ln1_bias, q_bias, v_bias, proj_bias, ln2_gain, ln2_bias, fc2_bias]
        side = jnp.concatenate(
            [v.reshape(R, 1) for v in vecs] + [fc1_bias.reshape(R, Q)], axis=1
        )
        side = jnp.pad(side, ((0, 0), (0, 128 - side.shape[1])))
        block = jnp.concatenate([proj_weight[0].T, side], axis=1)
        block = jnp.stack([block if k == 0 else swap(block, kz=k) for k in range(Z)])
        block = jnp.stack([block if k == 0 else swap(block, kf=k) for k in range(F)])
        block = jnp.stack([block, swap(block, kc=1)], axis=2)
        block = reorder(reorder(reorder(block, fi, 0), zi, 1), ci, 2).reshape(D, D + 128)
        proj_t = block[:, :D]
        side = block[:, D:].astype(f32)
        side_t = side[:, : len(vecs)].T
        gain_one, shift_one, bias_q, bias_v, proj_shift, gain_two, shift_two, down_shift = [
            side_t[i : i + 1] for i in range(len(vecs))
        ]
        up_shift = lax.dynamic_slice_in_dim(side, pi * (D // PL), D // PL, 0)
        up_shift = up_shift[:, len(vecs) : len(vecs) + Q].reshape(1, B)

        grad_low = grad_own.astype(bf16)
        grad_all = gather_plane(grad_low)

        w_ffn = jnp.concatenate(
            [fc1_weight[0].reshape(R, F, 1, 2, B), fc2_weight[0].T.reshape(R, F, 1, 2, B)], axis=4
        ).transpose(1, 2, 3, 0, 4)
        w_ffn = jnp.broadcast_to(w_ffn, (F, Z, 2, R, 2 * B)).reshape(N_DEV, R, 2 * B)
        w_ffn = exchange(w_ffn, ALL).reshape(D, 2 * B)
        w_up = w_ffn[:, :B]
        w_down_t = w_ffn[:, B:]

        valid_col = reorder(valid_mask[0].reshape(S, T), si).reshape(N, 1)
        normed_all, _ = normalize(x_all.astype(f32))
        attn_in = (normed_all * gain_one + shift_one).astype(bf16)
        qkv = mm(attn_in, w_qkv)
        my_cols = lambda vec: lax.dynamic_slice(vec, (0, si * W), (1, W))
        q = (qkv[:, :W] + my_cols(bias_q)).astype(bf16)
        k = qkv[:, W : 2 * W].astype(bf16)
        v = (qkv[:, 2 * W :] + my_cols(bias_v)).astype(bf16)
        mixed, logs = attn_fwd(q, k, v, valid_col)
        attended = exchange(reorder(mixed.reshape(S, T, W), si), SEQ)
        attended = attended.transpose(1, 0, 2).reshape(T, D)

        hidden = x_own.astype(f32)
        after_attn = hidden + mm(attended, proj_t, 1, 1) + proj_shift
        normed_two, spread_two = normalize(after_attn)
        mlp_in = (normed_two * gain_two + shift_two).astype(bf16)

        mlp_all = gather_plane(mlp_in)
        pre_act = mm(mlp_all, w_up) + up_shift
        erf_part = lax.erf(pre_act * root_half)
        activated = (0.5 * pre_act * (1.0 + erf_part)).astype(bf16)
        slope = 0.5 * (1.0 + erf_part) + pre_act * inv_root_tau * jnp.exp(-0.5 * pre_act * pre_act)
        pre_grad = mm(grad_all, w_down_t) * slope
        pre_low = pre_grad.astype(bf16)
        up_shift_grad = jnp.sum(pre_grad, axis=0)
        mlp_grad = scatter_sum(mm(pre_low, w_up, 1, 1), F, "kf")

        mid_grad = grad_own + norm_back(mlp_grad, normed_two, spread_two, gain_two)
        mid_low = mid_grad.astype(bf16)
        attended_grad = mm(mid_low, proj_t, 1, 0).astype(bf16)
        attended_grad = exchange(attended_grad.reshape(T, S, W).transpose(1, 0, 2), SEQ)
        attended_grad = reorder(attended_grad, si).reshape(N, W)

        down_out = scatter_sum(mm(activated, w_down_t, 1, 1), F, "kf")
        block_out = (after_attn + down_out + down_shift).astype(bf16)
        ffn_grad = jnp.concatenate(
            [mm(mlp_all, pre_low, 0, 0).astype(bf16), mm(grad_all, activated, 0, 0).astype(bf16)],
            axis=1,
        )
        ffn_grad = exchange(ffn_grad.reshape(N_DEV, R, 2 * B), ALL)
        ffn_grad = jnp.sum(ffn_grad.reshape(F, Z, 2, R, 2 * B).astype(f32), axis=1)
        up_grad = ffn_grad[..., :B].transpose(2, 0, 1, 3).reshape(1, R, FF)
        down_grad = ffn_grad[..., B:].transpose(0, 1, 3, 2).reshape(1, FF, R)

        proj_grad = mm(mid_low, attended, 0, 0).astype(bf16).reshape(N_DEV, R, D)
        proj_grad = jnp.sum(exchange(proj_grad, ALL).astype(f32), axis=0).T.reshape(1, D, R)

        dq, dk, dv = attn_bwd(q, attended_grad, logs, k, v, valid_col)
        qkv_grad = jnp.concatenate([dq, dk, dv], axis=1)
        attn_in_grad = mm(qkv_grad, w_qkv, 1, 1)
        gain_one_grad = jnp.sum(attn_in_grad * normed_all, axis=0)
        shift_one_grad = jnp.sum(attn_in_grad, axis=0)
        attn_in_grad = scatter_sum(attn_in_grad, Z, "kz")
        normed_one, spread_one = normalize(hidden)
        images_grad = mid_grad + norm_back(attn_in_grad, normed_one, spread_one, gain_one)

        w_grad = mm(attn_in, qkv_grad, 0, 0).astype(bf16).reshape(N_DEV, R, 3 * W)
        w_grad = exchange(w_grad, ALL).reshape(F, S, R, 3, W)
        w_grad = jnp.sum(w_grad.astype(f32), axis=0)
        qkv_weight_grad = w_grad.transpose(1, 2, 0, 3).reshape(1, R, 3 * D)

        my_slots = lambda part: lax.dynamic_update_slice(jnp.zeros((D,), f32), part, (si * W,))
        parts = [
            gain_one_grad,
            shift_one_grad,
            my_slots(jnp.sum(dq.astype(f32), axis=0)),
            my_slots(jnp.sum(dv.astype(f32), axis=0)),
            jnp.sum(mid_grad, axis=0),
            jnp.sum(mlp_grad * normed_two, axis=0),
            jnp.sum(mlp_grad, axis=0),
            jnp.sum(grad_own, axis=0),
            lax.dynamic_update_slice(jnp.zeros((FF,), f32), up_shift_grad, (pi * B,)),
        ]
        sums = jnp.concatenate([part.reshape(N_DEV, -1) for part in parts], axis=1)
        sums = jnp.sum(exchange(sums.reshape(N_DEV, 1, -1), ALL), axis=0)
        g = [sums[:, i * R : (i + 1) * R] for i in range(8)]
        return (
            block_out[None],
            images_grad[None],
            g[0],
            g[1],
            qkv_weight_grad,
            g[2],
            g[3],
            proj_grad,
            g[4],
            g[5],
            g[6],
            up_grad,
            sums[:, 8 * R :],
            down_grad,
            g[7],
        )

    return shards


def solution(mesh):
    F, S = mesh.shape["fsdp"], mesh.shape["seq"]
    Z = S // 2
    split = Mesh(mesh.devices.reshape(F, Z, 2), ALL)
    tok = P("fsdp", SEQ, None)
    vec = P(None, ALL)
    rows = P(None, ALL, None)
    cols = P(None, None, ALL)
    in_specs = (
        tok, P("fsdp", None), vec, vec, rows, vec, vec, cols, vec, vec, vec, rows, vec, cols, vec, tok,
    )
    out_specs = (tok, tok, vec, vec, rows, vec, vec, cols, vec, vec, vec, rows, vec, cols, vec)
    return jax.shard_map(
        make_shards(F, Z), mesh=split, in_specs=in_specs, out_specs=out_specs, check_vma=False
    )
```

```python
import jax
import jax.numpy as jnp
from jax import lax
from jax.experimental import pallas as pl
from jax.experimental.pallas import tpu as pltpu
from jax.sharding import Mesh
from jax.sharding import PartitionSpec as P


HD = 64

epsilon = 1e-06
masked_score = -1e30
root_half = 0.7071067811865476
inv_root_tau = 0.3989422804014327
f32 = jnp.float32
bf16 = jnp.bfloat16
ALL = ("fsdp", "z", "core")
SEQ = ("z", "core")


def normalize(hidden):
    center = hidden - jnp.mean(hidden, axis=-1, keepdims=True)
    spread = lax.rsqrt(jnp.mean(center * center, axis=-1, keepdims=True) + epsilon)
    return (center * spread, spread)


def norm_back(grad_in, normed, spread, gain_vec):
    scaled = grad_in * gain_vec
    return spread * (
        scaled
        - jnp.mean(scaled, axis=-1, keepdims=True)
        - normed * jnp.mean(scaled * normed, axis=-1, keepdims=True)
    )


def mm(a, b, ca=1, cb=0):
    return lax.dot_general(a, b, (((ca,), (cb,)), ((), ())), preferred_element_type=f32)


def lanes_of(block, head):
    lane = lax.broadcasted_iota(jnp.int32, block.shape, 1)
    return jnp.where(lane // HD == head, block, jnp.zeros_like(block))


def attn_fwd_body(one_ref, two_ref, ok_ref, out_ref, log_ref, all_ref):
    half = one_ref.shape[0]
    qb, width = out_ref.shape
    heads = width // HD
    step = pl.program_id(0)

    @pl.when(step == 0)
    def _():
        all_ref[:half] = one_ref[...]
        all_ref[half:] = two_ref[...]

    queries = all_ref[pl.ds(step * qb, qb), :width] * 0.125
    keys = all_ref[:, width : 2 * width]
    values = all_ref[:, 2 * width :]
    valid = ok_ref[...] > 0
    tops = []
    logs = []
    for head in range(heads):
        scores = mm(keys, lanes_of(queries, head), 1, 1)
        scores = jnp.where(valid, scores, masked_score)
        top = jnp.max(scores, axis=0, keepdims=True)
        powers = jnp.exp(scores - top)
        total = jnp.sum(powers, axis=0, keepdims=True)
        probs = (powers * (1.0 / total)).astype(bf16)
        mixed = mm(values, probs, 0, 0)
        tops.append(mixed[head * HD : (head + 1) * HD])
        logs.append(top + jnp.log(total))
    out_ref[...] = jnp.concatenate(tops, axis=0).T.astype(bf16)
    log_ref[...] = jnp.concatenate(logs, axis=0)


def attn_bwd_body(
    g_ref, log_ref, one_ref, two_ref, ok_ref, out_ref, sum_ref, all_ref, dk_acc, dv_acc
):
    half = one_ref.shape[0]
    qb, width = g_ref.shape
    heads = width // HD
    step = pl.program_id(0)

    @pl.when(step == 0)
    def _():
        all_ref[:half] = one_ref[...]
        all_ref[half:] = two_ref[...]
        dk_acc[...] = jnp.zeros_like(dk_acc)
        dv_acc[...] = jnp.zeros_like(dv_acc)

    queries = all_ref[pl.ds(step * qb, qb), :width] * 0.125
    keys = all_ref[:, width : 2 * width]
    values = all_ref[:, 2 * width :]
    grads = g_ref[...]
    valid = ok_ref[...] > 0
    logs = log_ref[...]
    parts = []
    key_sum = dk_acc[...]
    value_sum = dv_acc[...]
    for head in range(heads):
        q_head = lanes_of(queries, head)
        g_head = lanes_of(grads, head)
        scores = mm(keys, q_head, 1, 1)
        scores = jnp.where(valid, scores, masked_score)
        weights = jnp.exp(scores - logs[head : head + 1])
        prob_grad = mm(values, g_head, 1, 1)
        delta = jnp.sum(weights * prob_grad, axis=0, keepdims=True)
        score_grad = (weights * (prob_grad - delta)).astype(bf16)
        value_sum = value_sum + mm(weights.astype(bf16), g_head)
        key_sum = key_sum + mm(score_grad, q_head)
        mixed = mm(keys, score_grad, 0, 0)
        parts.append(mixed[head * HD : (head + 1) * HD])
    dk_acc[...] = key_sum
    dv_acc[...] = value_sum
    dq = (0.125 * jnp.concatenate(parts, axis=0).T).astype(bf16)
    out_ref[pl.ds(step * qb, qb), :width] = dq

    @pl.when(step == pl.num_programs(0) - 1)
    def _():
        out_ref[:, width : 2 * width] = dk_acc[...].astype(bf16)
        out_ref[:, 2 * width :] = dv_acc[...].astype(bf16)
        sum_ref[...] = jnp.sum(out_ref[...].astype(f32), axis=0, keepdims=True)


def attn_fwd(one, two, valid_col):
    n, w = valid_col.shape[0], one.shape[1] // 3
    heads = w // HD
    qb = min(256, n)
    whole = lambda i: (0, 0)
    return pl.pallas_call(
        attn_fwd_body,
        grid=(n // qb,),
        in_specs=[
            pl.BlockSpec((n // 2, 3 * w), whole),
            pl.BlockSpec((n // 2, 3 * w), whole),
            pl.BlockSpec((n, 1), whole),
        ],
        out_specs=[
            pl.BlockSpec((qb, w), lambda i: (i, 0)),
            pl.BlockSpec((heads, qb), lambda i: (0, i)),
        ],
        out_shape=[
            jax.ShapeDtypeStruct((n, w), bf16),
            jax.ShapeDtypeStruct((heads, n), f32),
        ],
        scratch_shapes=[pltpu.VMEM((n, 3 * w), bf16)],
        name="attn_fwd",
    )(one, two, valid_col)


def attn_bwd(grad, logs, one, two, valid_col):
    n, w = grad.shape
    heads = w // HD
    qb = min(256, n)
    whole = lambda i: (0, 0)
    return pl.pallas_call(
        attn_bwd_body,
        grid=(n // qb,),
        in_specs=[
            pl.BlockSpec((qb, w), lambda i: (i, 0)),
            pl.BlockSpec((heads, qb), lambda i: (0, i)),
            pl.BlockSpec((n // 2, 3 * w), whole),
            pl.BlockSpec((n // 2, 3 * w), whole),
            pl.BlockSpec((n, 1), whole),
        ],
        out_specs=[pl.BlockSpec((n, 3 * w), whole), pl.BlockSpec((1, 3 * w), whole)],
        out_shape=[
            jax.ShapeDtypeStruct((n, 3 * w), bf16),
            jax.ShapeDtypeStruct((1, 3 * w), f32),
        ],
        scratch_shapes=[
            pltpu.VMEM((n, 3 * w), bf16),
            pltpu.VMEM((n, w), f32),
            pltpu.VMEM((n, w), f32),
        ],
        name="attn_bwd",
    )(grad, logs, one, two, valid_col)


def make_shards(F, Z):
    S = 2 * Z
    N_DEV = F * S
    PL = 2 * F

    def swap(x, kf=0, kz=0, kc=0):
        pairs = []
        for f in range(F):
            for z in range(Z):
                for c in range(2):
                    src = (f * Z + z) * 2 + c
                    pairs.append((src, ((f ^ kf) * Z + (z ^ kz)) * 2 + (c ^ kc)))
        return lax.ppermute(x, ALL, pairs)

    def reorder(x, index, axis=0):
        size = x.shape[axis]
        shape = x.shape
        for bit in range(size.bit_length() - 1):
            low = 1 << bit
            split = x.reshape(shape[:axis] + (size // (2 * low), 2, low) + shape[axis + 1 :])
            flipped = jnp.flip(split, axis=axis + 1)
            x = jnp.where((index >> bit) & 1 == 1, flipped, split).reshape(shape)
        return x

    def gather_halves(x, outer, axis_name):
        blocks = [x]
        for k in range(1, outer):
            blocks.append(swap(x, **{axis_name: k}))
        mine = jnp.concatenate(blocks, axis=0)
        return mine, swap(mine, kc=1)

    def scatter_sum(mine, other, outer, axis_name):
        other = swap(other.astype(bf16), kc=1)
        mine = lax.optimization_barrier(mine)
        half = (mine + other.astype(f32)).astype(bf16)
        half = half.reshape(outer, -1, half.shape[-1])
        total = half[0].astype(f32)
        for k in range(1, outer):
            part = swap(half[k], **{axis_name: k})
            total = total + part.astype(f32)
        return total

    def place(block, count, axis_name, index, axis):
        shape = block.shape[:axis] + (count,) + block.shape[axis:]
        out = jnp.zeros(shape, block.dtype)
        for k in range(count):
            part = block if k == 0 else swap(block, **{axis_name: k})
            out = lax.dynamic_update_slice_in_dim(
                out, jnp.expand_dims(part, axis), index ^ k, axis
            )
        return out

    def reduce_over(x, count, axis_name, index, axis):
        total = lax.dynamic_index_in_dim(x, index, axis, keepdims=False).astype(f32)
        for k in range(1, count):
            part = lax.dynamic_index_in_dim(x, index ^ k, axis, keepdims=False)
            part = swap(part, **{axis_name: k})
            total = total + part.astype(f32)
        return total

    def exchange(x, axes):
        return lax.all_to_all(x, axes, split_axis=0, concat_axis=0, tiled=True)

    def shards(
        images,
        valid_mask,
        ln1_gain,
        ln1_bias,
        qkv_weight,
        q_bias,
        v_bias,
        proj_weight,
        proj_bias,
        ln2_gain,
        ln2_bias,
        fc1_weight,
        fc1_bias,
        fc2_weight,
        fc2_bias,
        out_grad,
    ):
        _, T, D = images.shape
        R = D // N_DEV
        FF = fc1_weight.shape[2]
        W = D // S
        B = FF // PL
        Q = FF // D
        N = S * T
        fi = lax.axis_index("fsdp")
        zi = lax.axis_index("z")
        ci = lax.axis_index("core")
        si = zi * 2 + ci
        pi = fi * 2 + ci

        x_own = images[0]
        grad_own = out_grad[0]
        x_halves = gather_halves(x_own, Z, "kz")

        w_qkv = qkv_weight[0].reshape(R, 3, S, W).transpose(2, 0, 1, 3).reshape(1, S, R, 3 * W)
        w_qkv = jnp.broadcast_to(w_qkv, (F, S, R, 3 * W)).reshape(N_DEV, R, 3 * W)
        w_qkv = exchange(w_qkv, ALL).reshape(D, 3 * W)

        vecs = [ln1_gain, ln1_bias, q_bias, v_bias, proj_bias, ln2_gain, ln2_bias, fc2_bias]
        side = jnp.concatenate(vecs + [fc1_bias.reshape(R, Q).T], axis=0)
        side = jnp.pad(side, ((0, 128 - side.shape[0]), (0, 0)))
        block = jnp.concatenate([proj_weight[0], side], axis=0).T
        block = place(block, Z, "kz", zi, 0)
        block = place(block, F, "kf", fi, 0)
        block = place(block, 2, "kc", ci, 2).reshape(D, D + 128)
        proj_t = block[:, :D]
        side = block[:, D:].astype(f32)
        side_t = side[:, : len(vecs)].T
        gain_one, shift_one, bias_q, bias_v, proj_shift, gain_two, shift_two, down_shift = [
            side_t[i : i + 1] for i in range(len(vecs))
        ]
        up_shift = lax.dynamic_slice_in_dim(side, pi * (D // PL), D // PL, 0)
        up_shift = up_shift[:, len(vecs) : len(vecs) + Q].reshape(1, B)

        w_ffn = jnp.concatenate(
            [fc1_weight[0].reshape(R, PL, B), fc2_weight[0].T.reshape(R, PL, B)], axis=2
        ).transpose(1, 0, 2)
        w_ffn = exchange(w_ffn, ("fsdp", "core")).reshape(F, 2, R, 2 * B)
        w_ffn = place(w_ffn, Z, "kz", zi, 1).reshape(D, 2 * B)
        w_up = w_ffn[:, :B]
        w_down_t = w_ffn[:, B:]

        grad_halves = gather_halves(grad_own.astype(bf16), F, "kf")

        valid_col = valid_mask[0].reshape(Z, 2, T).transpose(1, 0, 2)
        valid_col = reorder(reorder(valid_col, ci, 0), zi, 1).reshape(N, 1)
        my_cols = lambda vec: lax.dynamic_slice(vec, (0, si * W), (1, W))
        bias_row = jnp.concatenate([my_cols(bias_q), jnp.zeros((1, W), f32), my_cols(bias_v)], axis=1)
        normed_all, attn_in, qkv = [], [], []
        for part in x_halves:
            normed, _ = normalize(part.astype(f32))
            normed_all.append(normed)
            attn_in.append((normed * gain_one + shift_one).astype(bf16))
            qkv.append((mm(attn_in[-1], w_qkv) + bias_row).astype(bf16))
        mixed, logs = attn_fwd(qkv[0], qkv[1], valid_col)
        mixed = reorder(reorder(mixed.reshape(2, Z, T, W), ci, 0), zi, 1)
        mixed = mixed.transpose(1, 0, 2, 3).reshape(S, T, W)
        attended = exchange(mixed, SEQ)
        attended = attended.transpose(1, 0, 2).reshape(T, D)

        hidden = x_own.astype(f32)
        after_attn = hidden + mm(attended, proj_t, 1, 1) + proj_shift
        normed_two, spread_two = normalize(after_attn)
        mlp_in = (normed_two * gain_two + shift_two).astype(bf16)

        mlp_halves = gather_halves(mlp_in, F, "kf")
        activated, pre_low = [], []
        up_shift_grad = 0.0
        for mlp_part, grad_part in zip(mlp_halves, grad_halves):
            pre_act = mm(mlp_part, w_up) + up_shift
            erf_part = lax.erf(pre_act * root_half)
            activated.append((0.5 * pre_act * (1.0 + erf_part)).astype(bf16))
            slope = 0.5 * (1.0 + erf_part) + pre_act * inv_root_tau * jnp.exp(
                -0.5 * pre_act * pre_act
            )
            pre_grad = mm(grad_part, w_down_t) * slope
            pre_low.append(pre_grad.astype(bf16))
            up_shift_grad = up_shift_grad + jnp.sum(pre_grad, axis=0)
        mlp_grad = scatter_sum(mm(pre_low[0], w_up, 1, 1), mm(pre_low[1], w_up, 1, 1), F, "kf")

        ffn_grad = jnp.concatenate(
            [
                sum(mm(m, p, 0, 0) for m, p in zip(mlp_halves, pre_low)).astype(bf16),
                sum(mm(g, a, 0, 0) for g, a in zip(grad_halves, activated)).astype(bf16),
            ],
            axis=1,
        )
        ffn_grad = reduce_over(ffn_grad.reshape(F, Z, 2, R, 2 * B), Z, "kz", zi, 1)
        ffn_grad = exchange(ffn_grad.astype(bf16).reshape(PL, R, 2 * B), ("fsdp", "core"))
        ffn_grad = ffn_grad.astype(f32)
        up_grad = ffn_grad[..., :B].transpose(1, 0, 2).reshape(1, R, FF)
        down_grad = ffn_grad[..., B:].transpose(0, 2, 1).reshape(1, FF, R)
        mid_grad = grad_own + norm_back(mlp_grad, normed_two, spread_two, gain_two)
        mid_low = mid_grad.astype(bf16)
        mid_low, after_late, activated[0], activated[1] = lax.optimization_barrier(
            (mid_low, after_attn, activated[0], activated[1])
        )
        down_out = scatter_sum(
            mm(activated[0], w_down_t, 1, 1), mm(activated[1], w_down_t, 1, 1), F, "kf"
        )
        block_out = (after_late + down_out + down_shift).astype(bf16)

        attended_grad = mm(mid_low, proj_t, 1, 0).astype(bf16)
        attended_grad = exchange(attended_grad.reshape(T, S, W).transpose(1, 0, 2), SEQ)
        attended_grad = attended_grad.reshape(Z, 2, T, W).transpose(1, 0, 2, 3)
        attended_grad = reorder(reorder(attended_grad, ci, 0), zi, 1).reshape(N, W)

        proj_grad = mm(mid_low, attended, 0, 0).astype(bf16)
        proj_grad = reduce_over(proj_grad.reshape(F, Z, 2, R, D), 2, "kc", ci, 2)
        proj_grad = reduce_over(proj_grad.astype(bf16), F, "kf", fi, 0)
        proj_grad = reduce_over(proj_grad.astype(bf16), Z, "kz", zi, 0)
        proj_grad = proj_grad.T.reshape(1, D, R)

        qkv_grad, qkv_sums = attn_bwd(attended_grad, logs, qkv[0], qkv[1], valid_col)
        qkv_halves = (qkv_grad[: N // 2], qkv_grad[N // 2 :])
        in_grads = [mm(part, w_qkv, 1, 1) for part in qkv_halves]
        gain_one_grad = sum(jnp.sum(a * b, axis=0) for a, b in zip(in_grads, normed_all))
        shift_one_grad = sum(jnp.sum(a, axis=0) for a in in_grads)
        attn_in_grad = scatter_sum(in_grads[0], in_grads[1], Z, "kz")
        normed_one, spread_one = normalize(hidden)
        images_grad = mid_grad + norm_back(attn_in_grad, normed_one, spread_one, gain_one)

        w_grad = sum(mm(a, g, 0, 0) for a, g in zip(attn_in, qkv_halves)).astype(bf16)
        w_grad = reduce_over(w_grad.reshape(F, S, R, 3 * W), F, "kf", fi, 0)
        w_grad = exchange(w_grad.astype(bf16), SEQ).astype(f32)
        qkv_weight_grad = jnp.concatenate(
            [
                w_grad[..., i * W : (i + 1) * W].transpose(1, 0, 2).reshape(1, R, D)
                for i in range(3)
            ],
            axis=2,
        )

        my_slots = lambda part: lax.dynamic_update_slice(jnp.zeros((D,), f32), part, (si * W,))
        parts = [
            gain_one_grad,
            shift_one_grad,
            my_slots(qkv_sums[0, :W]),
            my_slots(qkv_sums[0, 2 * W :]),
            jnp.sum(mid_grad, axis=0),
            jnp.sum(mlp_grad * normed_two, axis=0),
            jnp.sum(mlp_grad, axis=0),
            jnp.sum(grad_own, axis=0),
            lax.dynamic_update_slice(jnp.zeros((FF,), f32), up_shift_grad, (pi * B,)),
        ]
        sums = jnp.concatenate([part.reshape(N_DEV, -1) for part in parts], axis=1)
        sums = exchange(sums.reshape(N_DEV, 1, -1), ALL)
        sums = jnp.sum(sums, axis=0)
        g = [sums[:, i * R : (i + 1) * R] for i in range(8)]
        return (
            block_out[None],
            images_grad[None],
            g[0],
            g[1],
            qkv_weight_grad,
            g[2],
            g[3],
            proj_grad,
            g[4],
            g[5],
            g[6],
            up_grad,
            sums[:, 8 * R :],
            down_grad,
            g[7],
        )

    return shards


def solution(mesh):
    F, S = mesh.shape["fsdp"], mesh.shape["seq"]
    Z = S // 2
    split = Mesh(mesh.devices.reshape(F, Z, 2), ALL)
    tok = P("fsdp", SEQ, None)
    vec = P(None, ALL)
    rows = P(None, ALL, None)
    cols = P(None, None, ALL)
    in_specs = (
        tok, P("fsdp", None), vec, vec, rows, vec, vec, cols, vec, vec, vec, rows, vec, cols, vec, tok,
    )
    out_specs = (tok, tok, vec, vec, rows, vec, vec, cols, vec, vec, vec, rows, vec, cols, vec)
    inner = make_shards(F, Z)

    return jax.shard_map(inner, mesh=split, in_specs=in_specs, out_specs=out_specs, check_vma=False)
```

```python
import jax
import jax.numpy as jnp
from jax import lax
from jax.experimental import pallas as pl
from jax.experimental.pallas import tpu as pltpu
from jax.sharding import Mesh
from jax.sharding import PartitionSpec as P


HD = 64

epsilon = 1e-06
masked_score = -1e30
root_half = 0.7071067811865476
inv_root_tau = 0.3989422804014327
f32 = jnp.float32
bf16 = jnp.bfloat16
ALL = ("fsdp", "z", "core")
SEQ = ("z", "core")


def normalize(hidden):
    center = hidden - jnp.mean(hidden, axis=-1, keepdims=True)
    spread = lax.rsqrt(jnp.mean(center * center, axis=-1, keepdims=True) + epsilon)
    return (center * spread, spread)


def norm_back(grad_in, normed, spread, gain_vec):
    scaled = grad_in * gain_vec
    return spread * (
        scaled
        - jnp.mean(scaled, axis=-1, keepdims=True)
        - normed * jnp.mean(scaled * normed, axis=-1, keepdims=True)
    )


def mm(a, b, ca=1, cb=0):
    return lax.dot_general(a, b, (((ca,), (cb,)), ((), ())), preferred_element_type=f32)


def lanes_of(block, head):
    lane = lax.broadcasted_iota(jnp.int32, block.shape, 1)
    return jnp.where(lane // HD == head, block, jnp.zeros_like(block))


def attn_fwd_body(one_ref, two_ref, ok_ref, out_ref, log_ref, all_ref):
    half = one_ref.shape[0]
    qb, width = out_ref.shape
    heads = width // HD
    step = pl.program_id(0)

    @pl.when(step == 0)
    def _():
        all_ref[:half] = one_ref[...]
        all_ref[half:] = two_ref[...]

    queries = all_ref[pl.ds(step * qb, qb), :width] * 0.125
    keys = all_ref[:, width : 2 * width]
    values = all_ref[:, 2 * width :]
    valid = ok_ref[...] > 0
    tops = []
    logs = []
    for head in range(heads):
        scores = mm(keys, lanes_of(queries, head), 1, 1)
        scores = jnp.where(valid, scores, masked_score)
        top = jnp.max(scores, axis=0, keepdims=True)
        powers = jnp.exp(scores - top)
        total = jnp.sum(powers, axis=0, keepdims=True)
        probs = (powers * (1.0 / total)).astype(bf16)
        mixed = mm(values, probs, 0, 0)
        tops.append(mixed[head * HD : (head + 1) * HD])
        logs.append(top + jnp.log(total))
    out_ref[...] = jnp.concatenate(tops, axis=0).T.astype(bf16)
    log_ref[...] = jnp.concatenate(logs, axis=0)


def attn_bwd_body(
    g_ref, log_ref, one_ref, two_ref, ok_ref, out_ref, sum_ref, all_ref, dk_acc, dv_acc
):
    half = one_ref.shape[0]
    qb, width = g_ref.shape
    heads = width // HD
    step = pl.program_id(0)

    @pl.when(step == 0)
    def _():
        all_ref[:half] = one_ref[...]
        all_ref[half:] = two_ref[...]
        dk_acc[...] = jnp.zeros_like(dk_acc)
        dv_acc[...] = jnp.zeros_like(dv_acc)

    queries = all_ref[pl.ds(step * qb, qb), :width] * 0.125
    keys = all_ref[:, width : 2 * width]
    values = all_ref[:, 2 * width :]
    grads = g_ref[...]
    valid = ok_ref[...] > 0
    logs = log_ref[...]
    parts = []
    key_sum = dk_acc[...]
    value_sum = dv_acc[...]
    for head in range(heads):
        q_head = lanes_of(queries, head)
        g_head = lanes_of(grads, head)
        scores = mm(keys, q_head, 1, 1)
        scores = jnp.where(valid, scores, masked_score)
        weights = jnp.exp(scores - logs[head : head + 1])
        prob_grad = mm(values, g_head, 1, 1)
        delta = jnp.sum(weights * prob_grad, axis=0, keepdims=True)
        score_grad = (weights * (prob_grad - delta)).astype(bf16)
        value_sum = value_sum + mm(weights.astype(bf16), g_head)
        key_sum = key_sum + mm(score_grad, q_head)
        mixed = mm(keys, score_grad, 0, 0)
        parts.append(mixed[head * HD : (head + 1) * HD])
    dk_acc[...] = key_sum
    dv_acc[...] = value_sum
    dq = (0.125 * jnp.concatenate(parts, axis=0).T).astype(bf16)
    out_ref[pl.ds(step * qb, qb), :width] = dq

    @pl.when(step == pl.num_programs(0) - 1)
    def _():
        out_ref[:, width : 2 * width] = dk_acc[...].astype(bf16)
        out_ref[:, 2 * width :] = dv_acc[...].astype(bf16)
        sum_ref[...] = jnp.sum(out_ref[...].astype(f32), axis=0, keepdims=True)


def attn_fwd(one, two, valid_col):
    n, w = valid_col.shape[0], one.shape[1] // 3
    heads = w // HD
    qb = min(256, n)
    whole = lambda i: (0, 0)
    return pl.pallas_call(
        attn_fwd_body,
        grid=(n // qb,),
        in_specs=[
            pl.BlockSpec((n // 2, 3 * w), whole),
            pl.BlockSpec((n // 2, 3 * w), whole),
            pl.BlockSpec((n, 1), whole),
        ],
        out_specs=[
            pl.BlockSpec((qb, w), lambda i: (i, 0)),
            pl.BlockSpec((heads, qb), lambda i: (0, i)),
        ],
        out_shape=[
            jax.ShapeDtypeStruct((n, w), bf16),
            jax.ShapeDtypeStruct((heads, n), f32),
        ],
        scratch_shapes=[pltpu.VMEM((n, 3 * w), bf16)],
        name="attn_fwd",
    )(one, two, valid_col)


def attn_bwd(grad, logs, one, two, valid_col):
    n, w = grad.shape
    heads = w // HD
    qb = min(256, n)
    whole = lambda i: (0, 0)
    return pl.pallas_call(
        attn_bwd_body,
        grid=(n // qb,),
        in_specs=[
            pl.BlockSpec((qb, w), lambda i: (i, 0)),
            pl.BlockSpec((heads, qb), lambda i: (0, i)),
            pl.BlockSpec((n // 2, 3 * w), whole),
            pl.BlockSpec((n // 2, 3 * w), whole),
            pl.BlockSpec((n, 1), whole),
        ],
        out_specs=[pl.BlockSpec((n, 3 * w), whole), pl.BlockSpec((1, 3 * w), whole)],
        out_shape=[
            jax.ShapeDtypeStruct((n, 3 * w), bf16),
            jax.ShapeDtypeStruct((1, 3 * w), f32),
        ],
        scratch_shapes=[
            pltpu.VMEM((n, 3 * w), bf16),
            pltpu.VMEM((n, w), f32),
            pltpu.VMEM((n, w), f32),
        ],
        name="attn_bwd",
    )(grad, logs, one, two, valid_col)


def ffn_grads_body(m0, m1, p0, p1, g0, g1, a0, a1, out_ref):
    blocks, _, rows, width = out_ref.shape
    hidden = width // 2
    up = mm(m0[...], p0[...], 0, 0) + mm(m1[...], p1[...], 0, 0)
    down = mm(g0[...], a0[...], 0, 0) + mm(g1[...], a1[...], 0, 0)
    for z in range(blocks):
        out_ref[z, 0, :, :hidden] = up[z * rows : (z + 1) * rows].astype(bf16)
        out_ref[z, 0, :, hidden:] = down[z * rows : (z + 1) * rows].astype(bf16)


def ffn_grads(mlp_halves, pre_low, grad_halves, activated, F, Z):
    tokens, D = mlp_halves[0].shape
    B = pre_low[0].shape[1]
    cols = pl.BlockSpec((tokens, D // F), lambda f: (0, f))
    whole = pl.BlockSpec((tokens, B), lambda f: (0, 0))
    rows = D // (F * Z)
    return pl.pallas_call(
        ffn_grads_body,
        grid=(F,),
        in_specs=[cols, cols, whole, whole] * 2,
        out_specs=pl.BlockSpec((Z, 1, rows, 2 * B), lambda f: (0, f, 0, 0)),
        out_shape=jax.ShapeDtypeStruct((Z, F, rows, 2 * B), bf16),
        name="ffn_grads",
    )(*mlp_halves, *pre_low, *grad_halves, *activated)


def make_shards(F, Z):
    S = 2 * Z
    N_DEV = F * S
    PL = 2 * F

    def swap(x, kf=0, kz=0, kc=0):
        pairs = []
        for f in range(F):
            for z in range(Z):
                for c in range(2):
                    src = (f * Z + z) * 2 + c
                    pairs.append((src, ((f ^ kf) * Z + (z ^ kz)) * 2 + (c ^ kc)))
        return lax.ppermute(x, ALL, pairs)

    def reorder(x, index, axis=0):
        size = x.shape[axis]
        shape = x.shape
        for bit in range(size.bit_length() - 1):
            low = 1 << bit
            split = x.reshape(shape[:axis] + (size // (2 * low), 2, low) + shape[axis + 1 :])
            flipped = jnp.flip(split, axis=axis + 1)
            x = jnp.where((index >> bit) & 1 == 1, flipped, split).reshape(shape)
        return x

    def gather_halves(x, outer, axis_name):
        blocks = [x]
        for k in range(1, outer):
            blocks.append(swap(x, **{axis_name: k}))
        mine = jnp.concatenate(blocks, axis=0)
        return mine, swap(mine, kc=1)

    def scatter_sum(mine, other, outer, axis_name):
        other = swap(other.astype(bf16), kc=1)
        mine = lax.optimization_barrier(mine)
        half = (mine + other.astype(f32)).astype(bf16)
        half = half.reshape(outer, -1, half.shape[-1])
        total = half[0].astype(f32)
        for k in range(1, outer):
            part = swap(half[k], **{axis_name: k})
            total = total + part.astype(f32)
        return total

    def place(block, count, axis_name, index, axis):
        shape = block.shape[:axis] + (count,) + block.shape[axis:]
        out = jnp.zeros(shape, block.dtype)
        for k in range(count):
            part = block if k == 0 else swap(block, **{axis_name: k})
            out = lax.dynamic_update_slice_in_dim(
                out, jnp.expand_dims(part, axis), index ^ k, axis
            )
        return out

    def reduce_over(x, count, axis_name, index, axis):
        total = lax.dynamic_index_in_dim(x, index, axis, keepdims=False).astype(f32)
        for k in range(1, count):
            part = lax.dynamic_index_in_dim(x, index ^ k, axis, keepdims=False)
            part = swap(part, **{axis_name: k})
            total = total + part.astype(f32)
        return total

    def exchange(x, axes):
        return lax.all_to_all(x, axes, split_axis=0, concat_axis=0, tiled=True)

    def shards(
        images,
        valid_mask,
        ln1_gain,
        ln1_bias,
        qkv_weight,
        q_bias,
        v_bias,
        proj_weight,
        proj_bias,
        ln2_gain,
        ln2_bias,
        fc1_weight,
        fc1_bias,
        fc2_weight,
        fc2_bias,
        out_grad,
    ):
        _, T, D = images.shape
        R = D // N_DEV
        FF = fc1_weight.shape[2]
        W = D // S
        B = FF // PL
        Q = FF // D
        N = S * T
        fi = lax.axis_index("fsdp")
        zi = lax.axis_index("z")
        ci = lax.axis_index("core")
        si = zi * 2 + ci
        pi = fi * 2 + ci

        x_own = images[0]
        grad_own = out_grad[0]
        x_halves = gather_halves(x_own, Z, "kz")

        vecs = [ln1_gain, ln1_bias, q_bias, v_bias, proj_bias, ln2_gain, ln2_bias, fc2_bias]
        count = len(vecs) + Q
        side = jnp.concatenate(vecs + [fc1_bias.reshape(Q, R)], axis=0)
        side = jnp.pad(side, ((0, -count % 16), (0, 3 * W - R)))
        w_qkv = qkv_weight[0].reshape(R, 3, S, W).transpose(2, 0, 1, 3).reshape(S, R, 3 * W)
        w_qkv = jnp.concatenate(
            [w_qkv, jnp.broadcast_to(side[None], (S,) + side.shape)], axis=1
        )
        w_qkv = exchange(w_qkv, SEQ)
        w_qkv = place(w_qkv, F, "kf", fi, 0)
        side = w_qkv[:, :, R : R + count, :R].astype(f32).reshape(N_DEV, count, R)
        w_qkv = w_qkv[:, :, :R].reshape(D, 3 * W)
        side_t = side[:, : len(vecs)].transpose(1, 0, 2).reshape(len(vecs), D)
        gain_one, shift_one, bias_q, bias_v, proj_shift, gain_two, shift_two, down_shift = [
            side_t[i : i + 1] for i in range(len(vecs))
        ]
        up_shift = lax.dynamic_slice_in_dim(side, pi * Z, Z, 0)[:, len(vecs) :].reshape(1, B)

        block = place(proj_weight[0].T, Z, "kz", zi, 0)
        block = place(block, F, "kf", fi, 0)
        proj_t = place(block, 2, "kc", ci, 2).reshape(D, D)

        w_ffn = jnp.concatenate(
            [fc1_weight[0].reshape(R, PL, B), fc2_weight[0].T.reshape(R, PL, B)], axis=2
        ).transpose(1, 0, 2)
        w_ffn = exchange(w_ffn, ("fsdp", "core")).reshape(F, 2, R, 2 * B)
        w_ffn = place(w_ffn, Z, "kz", zi, 1).reshape(D, 2 * B)
        w_up = w_ffn[:, :B]
        w_down_t = w_ffn[:, B:]

        grad_halves = gather_halves(grad_own.astype(bf16), F, "kf")

        valid_col = valid_mask[0].reshape(Z, 2, T).transpose(1, 0, 2)
        valid_col = reorder(reorder(valid_col, ci, 0), zi, 1).reshape(N, 1)
        my_cols = lambda vec: lax.dynamic_slice(vec, (0, si * W), (1, W))
        bias_row = jnp.concatenate([my_cols(bias_q), jnp.zeros((1, W), f32), my_cols(bias_v)], axis=1)
        normed_all, attn_in, qkv = [], [], []
        for part in x_halves:
            normed, _ = normalize(part.astype(f32))
            normed_all.append(normed)
            attn_in.append((normed * gain_one + shift_one).astype(bf16))
            qkv.append((mm(attn_in[-1], w_qkv) + bias_row).astype(bf16))
        mixed, logs = attn_fwd(qkv[0], qkv[1], valid_col)
        mixed = reorder(reorder(mixed.reshape(2, Z, T, W), ci, 0), zi, 1)
        mixed = mixed.transpose(1, 0, 2, 3).reshape(S, T, W)
        attended = exchange(mixed, SEQ)
        attended = attended.transpose(1, 0, 2).reshape(T, D)

        hidden = x_own.astype(f32)
        after_attn = hidden + mm(attended, proj_t, 1, 1) + proj_shift
        normed_two, spread_two = normalize(after_attn)
        mlp_in = (normed_two * gain_two + shift_two).astype(bf16)

        mlp_halves = gather_halves(mlp_in, F, "kf")
        activated, pre_low = [], []
        up_shift_grad = 0.0
        for mlp_part, grad_part in zip(mlp_halves, grad_halves):
            pre_act = mm(mlp_part, w_up) + up_shift
            erf_part = lax.erf(pre_act * root_half)
            activated.append((0.5 * pre_act * (1.0 + erf_part)).astype(bf16))
            slope = 0.5 * (1.0 + erf_part) + pre_act * inv_root_tau * jnp.exp(
                -0.5 * pre_act * pre_act
            )
            pre_grad = mm(grad_part, w_down_t) * slope
            pre_low.append(pre_grad.astype(bf16))
            up_shift_grad = up_shift_grad + jnp.sum(pre_grad, axis=0)
        mlp_part = mm(pre_low[0], w_up, 1, 1)
        mlp_grad = scatter_sum(mlp_part, mm(pre_low[1], w_up, 1, 1), F, "kf")

        ffn_grad = ffn_grads(mlp_halves, pre_low, grad_halves, activated, F, Z)
        ffn_grad = reduce_over(ffn_grad, Z, "kz", zi, 0)
        ffn_grad = exchange(ffn_grad.astype(bf16).reshape(PL, R, 2 * B), ("fsdp", "core"))
        ffn_grad = ffn_grad.astype(f32)
        up_grad = ffn_grad[..., :B].transpose(1, 0, 2).reshape(1, R, FF)
        down_grad = ffn_grad[..., B:].transpose(0, 2, 1).reshape(1, FF, R)
        mid_grad = grad_own + norm_back(mlp_grad, normed_two, spread_two, gain_two)
        mid_low = mid_grad.astype(bf16)
        mid_low, after_late, activated[0], activated[1] = lax.optimization_barrier(
            (mid_low, after_attn, activated[0], activated[1])
        )
        down_out = scatter_sum(
            mm(activated[0], w_down_t, 1, 1), mm(activated[1], w_down_t, 1, 1), F, "kf"
        )
        block_out = (after_late + down_out + down_shift).astype(bf16)

        attended_grad = mm(mid_low, proj_t, 1, 0).astype(bf16)
        attended_grad = exchange(attended_grad.reshape(T, S, W).transpose(1, 0, 2), SEQ)
        attended_grad = attended_grad.reshape(Z, 2, T, W).transpose(1, 0, 2, 3)
        attended_grad = reorder(reorder(attended_grad, ci, 0), zi, 1).reshape(N, W)

        proj_grad = mm(mid_low, attended, 0, 0).astype(bf16)
        proj_grad = reduce_over(proj_grad.reshape(F, Z, 2, R, D), 2, "kc", ci, 2)
        proj_grad = reduce_over(proj_grad.astype(bf16), F, "kf", fi, 0)
        proj_grad = reduce_over(proj_grad.astype(bf16), Z, "kz", zi, 0)
        proj_grad = proj_grad.T.reshape(1, D, R)

        qkv_grad, qkv_sums = attn_bwd(attended_grad, logs, qkv[0], qkv[1], valid_col)
        qkv_halves = (qkv_grad[: N // 2], qkv_grad[N // 2 :])
        in_late = mm(qkv_halves[1], w_qkv, 1, 1)
        late_low, first = lax.optimization_barrier((in_late.astype(bf16), qkv_halves[0]))
        in_grads = [mm(first, w_qkv, 1, 1), in_late]
        gain_one_grad = sum(jnp.sum(a * b, axis=0) for a, b in zip(in_grads, normed_all))
        shift_one_grad = sum(jnp.sum(a, axis=0) for a in in_grads)
        attn_in_grad = scatter_sum(in_grads[0], late_low, Z, "kz")
        normed_one, spread_one = normalize(hidden)
        images_grad = mid_grad + norm_back(attn_in_grad, normed_one, spread_one, gain_one)

        w_grad = sum(mm(a, g, 0, 0) for a, g in zip(attn_in, qkv_halves)).astype(bf16)
        w_grad = reduce_over(w_grad.reshape(F, S, R, 3 * W), F, "kf", fi, 0)
        w_grad = exchange(w_grad.astype(bf16), SEQ).astype(f32)
        qkv_weight_grad = jnp.concatenate(
            [
                w_grad[..., i * W : (i + 1) * W].transpose(1, 0, 2).reshape(1, R, D)
                for i in range(3)
            ],
            axis=2,
        )

        my_slots = lambda part: lax.dynamic_update_slice(jnp.zeros((D,), f32), part, (si * W,))
        parts = [
            gain_one_grad,
            shift_one_grad,
            my_slots(qkv_sums[0, :W]),
            my_slots(qkv_sums[0, 2 * W :]),
            jnp.sum(mid_grad, axis=0),
            jnp.sum(mlp_grad * normed_two, axis=0),
            jnp.sum(mlp_grad, axis=0),
            jnp.sum(grad_own, axis=0),
            lax.dynamic_update_slice(jnp.zeros((FF,), f32), up_shift_grad, (pi * B,)),
        ]
        sums = jnp.concatenate([part.reshape(N_DEV, -1) for part in parts], axis=1)
        sums = exchange(sums.reshape(N_DEV, 1, -1), ALL)
        sums = jnp.sum(sums, axis=0)
        g = [sums[:, i * R : (i + 1) * R] for i in range(8)]
        return (
            block_out[None],
            images_grad[None],
            g[0],
            g[1],
            qkv_weight_grad,
            g[2],
            g[3],
            proj_grad,
            g[4],
            g[5],
            g[6],
            up_grad,
            sums[:, 8 * R :],
            down_grad,
            g[7],
        )

    return shards


def solution(mesh):
    F, S = mesh.shape["fsdp"], mesh.shape["seq"]
    Z = S // 2
    split = Mesh(mesh.devices.reshape(F, Z, 2), ALL)
    tok = P("fsdp", SEQ, None)
    vec = P(None, ALL)
    rows = P(None, ALL, None)
    cols = P(None, None, ALL)
    in_specs = (
        tok, P("fsdp", None), vec, vec, rows, vec, vec, cols, vec, vec, vec, rows, vec, cols, vec, tok,
    )
    out_specs = (tok, tok, vec, vec, rows, vec, vec, cols, vec, vec, vec, rows, vec, cols, vec)
    inner = make_shards(F, Z)

    return jax.shard_map(inner, mesh=split, in_specs=in_specs, out_specs=out_specs, check_vma=False)
```

```python
import jax
import jax.numpy as jnp
from jax import lax
from jax.experimental import pallas as pl
from jax.experimental.pallas import tpu as pltpu
from jax.sharding import Mesh
from jax.sharding import PartitionSpec as P


HD = 64

epsilon = 1e-06
masked_score = -1e30
root_half = 0.7071067811865476
inv_root_tau = 0.3989422804014327
f32 = jnp.float32
bf16 = jnp.bfloat16
ALL = ("fsdp", "z", "core")
SEQ = ("z", "core")


def normalize(hidden):
    center = hidden - jnp.mean(hidden, axis=-1, keepdims=True)
    spread = lax.rsqrt(jnp.mean(center * center, axis=-1, keepdims=True) + epsilon)
    return (center * spread, spread)


def norm_back(grad_in, normed, spread, gain_vec):
    scaled = grad_in * gain_vec
    return spread * (
        scaled
        - jnp.mean(scaled, axis=-1, keepdims=True)
        - normed * jnp.mean(scaled * normed, axis=-1, keepdims=True)
    )


def mm(a, b, ca=1, cb=0):
    return lax.dot_general(a, b, (((ca,), (cb,)), ((), ())), preferred_element_type=f32)


def lanes_of(block, head):
    lane = lax.broadcasted_iota(jnp.int32, block.shape, 1)
    return jnp.where(lane // HD == head, block, jnp.zeros_like(block))


def attn_fwd_body(one_ref, two_ref, ok_ref, out_ref, log_ref, all_ref):
    half = one_ref.shape[0]
    qb, width = out_ref.shape
    heads = width // HD
    step = pl.program_id(0)

    @pl.when(step == 0)
    def _():
        all_ref[:half] = one_ref[...]
        all_ref[half:] = two_ref[...]

    queries = all_ref[pl.ds(step * qb, qb), :width] * 0.125
    keys = all_ref[:, width : 2 * width]
    values = all_ref[:, 2 * width :]
    valid = ok_ref[...] > 0
    tops = []
    logs = []
    for head in range(heads):
        scores = mm(keys, lanes_of(queries, head), 1, 1)
        scores = jnp.where(valid, scores, masked_score)
        top = jnp.max(scores, axis=0, keepdims=True)
        powers = jnp.exp(scores - top)
        total = jnp.sum(powers, axis=0, keepdims=True)
        probs = (powers * (1.0 / total)).astype(bf16)
        mixed = mm(values, probs, 0, 0)
        tops.append(mixed[head * HD : (head + 1) * HD])
        logs.append(top + jnp.log(total))
    out_ref[...] = jnp.concatenate(tops, axis=0).T.astype(bf16)
    log_ref[...] = jnp.concatenate(logs, axis=0)


def attn_bwd_body(
    g_ref, log_ref, one_ref, two_ref, ok_ref, d_one, d_two, sum_ref, all_ref, dk_acc, dv_acc
):
    half = one_ref.shape[0]
    qb, width = g_ref.shape
    heads = width // HD
    step = pl.program_id(0)

    @pl.when(step == 0)
    def _():
        all_ref[:half] = one_ref[...]
        all_ref[half:] = two_ref[...]
        dk_acc[...] = jnp.zeros_like(dk_acc)
        dv_acc[...] = jnp.zeros_like(dv_acc)

    queries = all_ref[pl.ds(step * qb, qb), :width] * 0.125
    keys = all_ref[:, width : 2 * width]
    values = all_ref[:, 2 * width :]
    grads = g_ref[...]
    valid = ok_ref[...] > 0
    logs = log_ref[...]
    parts = []
    key_sum = dk_acc[...]
    value_sum = dv_acc[...]
    for head in range(heads):
        q_head = lanes_of(queries, head)
        g_head = lanes_of(grads, head)
        scores = mm(keys, q_head, 1, 1)
        scores = jnp.where(valid, scores, masked_score)
        weights = jnp.exp(scores - logs[head : head + 1])
        prob_grad = mm(values, g_head, 1, 1)
        delta = jnp.sum(weights * prob_grad, axis=0, keepdims=True)
        score_grad = (weights * (prob_grad - delta)).astype(bf16)
        value_sum = value_sum + mm(weights.astype(bf16), g_head)
        key_sum = key_sum + mm(score_grad, q_head)
        mixed = mm(keys, score_grad, 0, 0)
        parts.append(mixed[head * HD : (head + 1) * HD])
    dk_acc[...] = key_sum
    dv_acc[...] = value_sum
    dq = (0.125 * jnp.concatenate(parts, axis=0).T).astype(bf16)
    all_ref[pl.ds(step * qb, qb), :width] = dq

    @pl.when(step == pl.num_programs(0) - 1)
    def _():
        all_ref[:, width : 2 * width] = dk_acc[...].astype(bf16)
        all_ref[:, 2 * width :] = dv_acc[...].astype(bf16)
        d_one[...] = all_ref[:half]
        d_two[...] = all_ref[half:]
        sum_ref[...] = jnp.sum(all_ref[...].astype(f32), axis=0, keepdims=True)


def attn_fwd(one, two, valid_col):
    n, w = valid_col.shape[0], one.shape[1] // 3
    heads = w // HD
    qb = min(128, n)
    whole = lambda i: (0, 0)
    return pl.pallas_call(
        attn_fwd_body,
        grid=(n // qb,),
        in_specs=[
            pl.BlockSpec((n // 2, 3 * w), whole),
            pl.BlockSpec((n // 2, 3 * w), whole),
            pl.BlockSpec((n, 1), whole),
        ],
        out_specs=[
            pl.BlockSpec((qb, w), lambda i: (i, 0)),
            pl.BlockSpec((heads, qb), lambda i: (0, i)),
        ],
        out_shape=[
            jax.ShapeDtypeStruct((n, w), bf16),
            jax.ShapeDtypeStruct((heads, n), f32),
        ],
        scratch_shapes=[pltpu.VMEM((n, 3 * w), bf16)],
        name="attn_fwd",
    )(one, two, valid_col)


def attn_bwd(grad, logs, one, two, valid_col):
    n, w = grad.shape
    heads = w // HD
    qb = min(256, n)
    whole = lambda i: (0, 0)
    return pl.pallas_call(
        attn_bwd_body,
        grid=(n // qb,),
        in_specs=[
            pl.BlockSpec((qb, w), lambda i: (i, 0)),
            pl.BlockSpec((heads, qb), lambda i: (0, i)),
            pl.BlockSpec((n // 2, 3 * w), whole),
            pl.BlockSpec((n // 2, 3 * w), whole),
            pl.BlockSpec((n, 1), whole),
        ],
        out_specs=[
            pl.BlockSpec((n // 2, 3 * w), whole),
            pl.BlockSpec((n // 2, 3 * w), whole),
            pl.BlockSpec((1, 3 * w), whole),
        ],
        out_shape=[
            jax.ShapeDtypeStruct((n // 2, 3 * w), bf16),
            jax.ShapeDtypeStruct((n // 2, 3 * w), bf16),
            jax.ShapeDtypeStruct((1, 3 * w), f32),
        ],
        scratch_shapes=[
            pltpu.VMEM((n, 3 * w), bf16),
            pltpu.VMEM((n, w), f32),
            pltpu.VMEM((n, w), f32),
        ],
        name="attn_bwd",
    )(grad, logs, one, two, valid_col)


def ffn_grads_body(m0, m1, p0, p1, g0, g1, a0, a1, out_ref):
    blocks, _, rows, width = out_ref.shape
    hidden = width // 2
    up = mm(m0[...], p0[...], 0, 0) + mm(m1[...], p1[...], 0, 0)
    down = mm(g0[...], a0[...], 0, 0) + mm(g1[...], a1[...], 0, 0)
    for z in range(blocks):
        out_ref[z, 0, :, :hidden] = up[z * rows : (z + 1) * rows].astype(bf16)
        out_ref[z, 0, :, hidden:] = down[z * rows : (z + 1) * rows].astype(bf16)


def ffn_grads(mlp_halves, pre_low, grad_halves, activated, F, Z):
    tokens, D = mlp_halves[0].shape
    B = pre_low[0].shape[1]
    cols = pl.BlockSpec((tokens, D // F), lambda f: (0, f))
    whole = pl.BlockSpec((tokens, B), lambda f: (0, 0))
    rows = D // (F * Z)
    return pl.pallas_call(
        ffn_grads_body,
        grid=(F,),
        in_specs=[cols, cols, whole, whole] * 2,
        out_specs=pl.BlockSpec((Z, 1, rows, 2 * B), lambda f: (0, f, 0, 0)),
        out_shape=jax.ShapeDtypeStruct((Z, F, rows, 2 * B), bf16),
        name="ffn_grads",
    )(*mlp_halves, *pre_low, *grad_halves, *activated)


def make_shards(F, Z):
    S = 2 * Z
    N_DEV = F * S
    PL = 2 * F

    def swap(x, kf=0, kz=0, kc=0):
        pairs = []
        for f in range(F):
            for z in range(Z):
                for c in range(2):
                    src = (f * Z + z) * 2 + c
                    pairs.append((src, ((f ^ kf) * Z + (z ^ kz)) * 2 + (c ^ kc)))
        return lax.ppermute(x, ALL, pairs)

    def reorder(x, index, axis=0):
        size = x.shape[axis]
        shape = x.shape
        for bit in range(size.bit_length() - 1):
            low = 1 << bit
            split = x.reshape(shape[:axis] + (size // (2 * low), 2, low) + shape[axis + 1 :])
            flipped = jnp.flip(split, axis=axis + 1)
            x = jnp.where((index >> bit) & 1 == 1, flipped, split).reshape(shape)
        return x

    def gather_halves(x, outer, axis_name):
        blocks = [x]
        for k in range(1, outer):
            blocks.append(swap(x, **{axis_name: k}))
        mine = jnp.concatenate(blocks, axis=0)
        return mine, swap(mine, kc=1)

    def scatter_sum(mine, other, outer, axis_name):
        other = swap(other.astype(bf16), kc=1)
        mine = lax.optimization_barrier(mine)
        half = (mine + other.astype(f32)).astype(bf16)
        half = half.reshape(outer, -1, half.shape[-1])
        total = half[0].astype(f32)
        for k in range(1, outer):
            part = swap(half[k], **{axis_name: k})
            total = total + part.astype(f32)
        return total

    def place(block, count, axis_name, index, axis):
        shape = block.shape[:axis] + (count,) + block.shape[axis:]
        out = jnp.zeros(shape, block.dtype)
        for k in range(count):
            part = block if k == 0 else swap(block, **{axis_name: k})
            out = lax.dynamic_update_slice_in_dim(out, jnp.expand_dims(part, axis), index ^ k, axis)
        return out

    def reduce_over(x, count, axis_name, index, axis):
        total = lax.dynamic_index_in_dim(x, index, axis, keepdims=False).astype(f32)
        for k in range(1, count):
            part = lax.dynamic_index_in_dim(x, index ^ k, axis, keepdims=False)
            part = swap(part, **{axis_name: k})
            total = total + part.astype(f32)
        return total

    def exchange(x, axes):
        return lax.all_to_all(x, axes, split_axis=0, concat_axis=0, tiled=True)

    def shards(
        images,
        valid_mask,
        ln1_gain,
        ln1_bias,
        qkv_weight,
        q_bias,
        v_bias,
        proj_weight,
        proj_bias,
        ln2_gain,
        ln2_bias,
        fc1_weight,
        fc1_bias,
        fc2_weight,
        fc2_bias,
        out_grad,
    ):
        _, T, D = images.shape
        R = D // N_DEV
        FF = fc1_weight.shape[2]
        W = D // S
        B = FF // PL
        Q = FF // D
        N = S * T
        fi = lax.axis_index("fsdp")
        zi = lax.axis_index("z")
        ci = lax.axis_index("core")
        si = zi * 2 + ci
        pi = fi * 2 + ci

        x_own = images[0]
        grad_own = out_grad[0]
        x_halves = gather_halves(x_own, Z, "kz")

        vecs = [ln1_gain, ln1_bias, q_bias, v_bias, proj_bias, ln2_gain, ln2_bias, fc2_bias]
        count = len(vecs) + Q
        side = jnp.concatenate(vecs + [fc1_bias.reshape(Q, R)], axis=0)
        side = jnp.pad(side, ((0, -count % 16), (0, 3 * W - R)))
        w_qkv = qkv_weight[0].reshape(R, 3, S, W).transpose(2, 0, 1, 3).reshape(S, R, 3 * W)
        w_qkv = jnp.concatenate(
            [w_qkv, jnp.broadcast_to(side[None], (S,) + side.shape)], axis=1
        )
        w_qkv = exchange(w_qkv, SEQ)
        w_qkv = place(w_qkv, F, "kf", fi, 0)
        side = w_qkv[:, :, R : R + count, :R].astype(f32).reshape(N_DEV, count, R)
        w_qkv = w_qkv[:, :, :R].reshape(D, 3 * W)
        side_t = side[:, : len(vecs)].transpose(1, 0, 2).reshape(len(vecs), D)
        gain_one, shift_one, bias_q, bias_v, proj_shift, gain_two, shift_two, down_shift = [
            side_t[i : i + 1] for i in range(len(vecs))
        ]
        up_shift = lax.dynamic_slice_in_dim(side, pi * Z, Z, 0)[:, len(vecs) :].reshape(1, B)

        block = place(proj_weight[0].T, Z, "kz", zi, 0)
        block = place(block, F, "kf", fi, 0)
        proj_t = place(block, 2, "kc", ci, 2).reshape(D, D)

        w_ffn = jnp.concatenate(
            [fc1_weight[0].reshape(R, PL, B), fc2_weight[0].T.reshape(R, PL, B)], axis=2
        ).transpose(1, 0, 2)
        w_ffn = exchange(w_ffn, ("fsdp", "core")).reshape(F, 2, R, 2 * B)
        w_ffn = place(w_ffn, Z, "kz", zi, 1).reshape(D, 2 * B)
        w_up = w_ffn[:, :B]
        w_down_t = w_ffn[:, B:]

        grad_halves = gather_halves(grad_own.astype(bf16), F, "kf")

        valid_col = valid_mask[0].reshape(Z, 2, T).transpose(1, 0, 2)
        valid_col = reorder(reorder(valid_col, ci, 0), zi, 1).reshape(N, 1)
        my_cols = lambda vec: lax.dynamic_slice(vec, (0, si * W), (1, W))
        bias_row = jnp.concatenate([my_cols(bias_q), jnp.zeros((1, W), f32), my_cols(bias_v)], axis=1)
        normed_all, attn_in, qkv = [], [], []
        for part in x_halves:
            normed, _ = normalize(part.astype(f32))
            normed_all.append(normed)
            attn_in.append((normed * gain_one + shift_one).astype(bf16))
            qkv.append((mm(attn_in[-1], w_qkv) + bias_row).astype(bf16))
        mixed, logs = attn_fwd(qkv[0], qkv[1], valid_col)
        mixed = reorder(reorder(mixed.reshape(2, Z, T, W), ci, 0), zi, 1)
        mixed = mixed.transpose(1, 0, 2, 3).reshape(S, T, W)
        attended = exchange(mixed, SEQ)
        attended = attended.transpose(1, 0, 2).reshape(T, D)

        hidden = x_own.astype(f32)
        after_attn = hidden + mm(attended, proj_t, 1, 1) + proj_shift
        normed_two, spread_two = normalize(after_attn)
        mlp_in = (normed_two * gain_two + shift_two).astype(bf16)

        mlp_halves = gather_halves(mlp_in, F, "kf")
        activated, pre_low = [], []
        up_shift_grad = 0.0
        for mlp_part, grad_part in zip(mlp_halves, grad_halves):
            pre_act = mm(mlp_part, w_up) + up_shift
            erf_part = lax.erf(pre_act * root_half)
            activated.append((0.5 * pre_act * (1.0 + erf_part)).astype(bf16))
            slope = 0.5 * (1.0 + erf_part) + pre_act * inv_root_tau * jnp.exp(
                -0.5 * pre_act * pre_act
            )
            pre_grad = mm(grad_part, w_down_t) * slope
            pre_low.append(pre_grad.astype(bf16))
            up_shift_grad = up_shift_grad + jnp.sum(pre_grad, axis=0)
        mlp_part = mm(pre_low[0], w_up, 1, 1)
        mlp_grad = scatter_sum(mlp_part, mm(pre_low[1], w_up, 1, 1), F, "kf")

        ffn_grad = ffn_grads(mlp_halves, pre_low, grad_halves, activated, F, Z)
        ffn_grad = reduce_over(ffn_grad, Z, "kz", zi, 0)
        ffn_grad = exchange(ffn_grad.astype(bf16).reshape(PL, R, 2 * B), ("fsdp", "core"))
        ffn_grad = ffn_grad.astype(f32)
        up_grad = ffn_grad[..., :B].transpose(1, 0, 2).reshape(1, R, FF)
        down_grad = ffn_grad[..., B:].transpose(0, 2, 1).reshape(1, FF, R)
        mid_grad = grad_own + norm_back(mlp_grad, normed_two, spread_two, gain_two)
        mid_low = mid_grad.astype(bf16)
        mid_low, after_late, activated[0], activated[1] = lax.optimization_barrier(
            (mid_low, after_attn, activated[0], activated[1])
        )
        down_out = scatter_sum(
            mm(activated[0], w_down_t, 1, 1), mm(activated[1], w_down_t, 1, 1), F, "kf"
        )
        block_out = (after_late + down_out + down_shift).astype(bf16)

        attended_grad = mm(mid_low, proj_t, 1, 0).astype(bf16)
        attended_grad = exchange(attended_grad.reshape(T, S, W).transpose(1, 0, 2), SEQ)
        attended_grad = attended_grad.reshape(Z, 2, T, W).transpose(1, 0, 2, 3)
        attended_grad = reorder(reorder(attended_grad, ci, 0), zi, 1).reshape(N, W)

        proj_grad = mm(mid_low, attended, 0, 0).astype(bf16)
        proj_grad = reduce_over(proj_grad.reshape(F, Z, 2, R, D), 2, "kc", ci, 2)
        proj_grad = lax.optimization_barrier(proj_grad.astype(bf16))
        proj_grad = reduce_over(proj_grad, F, "kf", fi, 0)
        proj_grad = reduce_over(proj_grad.astype(bf16), Z, "kz", zi, 0)
        proj_grad = proj_grad.T.reshape(1, D, R)

        *qkv_halves, qkv_sums = attn_bwd(attended_grad, logs, qkv[0], qkv[1], valid_col)
        in_late = mm(qkv_halves[1], w_qkv, 1, 1)
        in_late, late_low, first = lax.optimization_barrier(
            (in_late, in_late.astype(bf16), qkv_halves[0])
        )
        in_grads = [lax.optimization_barrier(mm(first, w_qkv, 1, 1)), in_late]
        gain_one_grad = sum(jnp.sum(a * b, axis=0) for a, b in zip(in_grads, normed_all))
        shift_one_grad = sum(jnp.sum(a, axis=0) for a in in_grads)
        attn_in_grad = scatter_sum(in_grads[0], late_low, Z, "kz")
        normed_one, spread_one = normalize(hidden)
        images_grad = mid_grad + norm_back(attn_in_grad, normed_one, spread_one, gain_one)

        w_grad = sum(mm(a, g, 0, 0) for a, g in zip(attn_in, qkv_halves)).astype(bf16)
        my_slots = lambda part: lax.dynamic_update_slice(jnp.zeros((D,), f32), part, (si * W,))
        parts = [
            gain_one_grad,
            shift_one_grad,
            my_slots(qkv_sums[0, :W]),
            my_slots(qkv_sums[0, 2 * W :]),
            jnp.sum(mid_grad, axis=0),
            jnp.sum(mlp_grad * normed_two, axis=0),
            jnp.sum(mlp_grad, axis=0),
            jnp.sum(grad_own, axis=0),
            lax.dynamic_update_slice(jnp.zeros((FF,), f32), up_shift_grad, (pi * B,)),
        ]
        sums = jnp.concatenate([part.reshape(N_DEV, -1) for part in parts], axis=1)
        sums = jnp.pad(sums.astype(bf16), ((0, 0), (0, 3 * W - sums.shape[1])))
        sums = jnp.pad(sums.reshape(F, S, 1, 3 * W), ((0, 0), (0, 0), (0, 15), (0, 0)))
        w_grad = jnp.concatenate([w_grad.reshape(F, S, R, 3 * W), sums], axis=2)
        w_grad = reduce_over(w_grad, F, "kf", fi, 0)
        w_grad = exchange(w_grad.astype(bf16), SEQ)
        sums = jnp.sum(w_grad[:, R].astype(f32), axis=0, keepdims=True)[:, : (8 + Q) * R]
        w_grad = w_grad[:, :R].astype(f32)
        qkv_weight_grad = jnp.concatenate(
            [
                w_grad[..., i * W : (i + 1) * W].transpose(1, 0, 2).reshape(1, R, D)
                for i in range(3)
            ],
            axis=2,
        )

        g = [sums[:, i * R : (i + 1) * R] for i in range(8)]
        return (
            block_out[None],
            images_grad[None],
            g[0],
            g[1],
            qkv_weight_grad,
            g[2],
            g[3],
            proj_grad,
            g[4],
            g[5],
            g[6],
            up_grad,
            sums[:, 8 * R :],
            down_grad,
            g[7],
        )

    return shards


def solution(mesh):
    F, S = mesh.shape["fsdp"], mesh.shape["seq"]
    Z = S // 2
    split = Mesh(mesh.devices.reshape(F, Z, 2), ALL)
    tok = P("fsdp", SEQ, None)
    vec = P(None, ALL)
    rows = P(None, ALL, None)
    cols = P(None, None, ALL)
    in_specs = (
        tok, P("fsdp", None), vec, vec, rows, vec, vec, cols, vec, vec, vec, rows, vec, cols, vec, tok,
    )
    out_specs = (tok, tok, vec, vec, rows, vec, vec, cols, vec, vec, vec, rows, vec, cols, vec)
    inner = make_shards(F, Z)

    return jax.shard_map(inner, mesh=split, in_specs=in_specs, out_specs=out_specs, check_vma=False)
```
